512 devices in a mesh: mem: 8 (over x, core), par: 64 (over y, z).
Axes of the slice: x: 4, y: 8, z: 8, core: 2. Of those that a mesh axis runs over, the one named last changes fastest.
Arguments:
- operator: float32 [131072, 512], P('par'), may hold values from -0.046875 to 0.046875
- ensemble: float32 [256, 131072], P('mem', 'par'), may hold values from -6 to 6
- noise: float32 [256, 512], P('mem'), may hold values from -6 to 6
- observations: float32 [16384], replicated, may hold values from -6 to 6
- variances: float32 [16384], replicated, may hold values from 0.25 to 4
- rows: int32 [512], replicated, may hold values from 0 to 16383
Outputs:
- updated: float32 [256, 131072], P('mem', 'par')
The draws below stay inside these ranges and needn't reach their ends.
Inputs may be any that keep to these rules, and one draw needn't show every extreme that they name: `rows`: indices into the observations; they may repeat.
All inputs are finite; a program needn't handle non-finite values.
Results may differ from the reference program's by a relative error of at most 0.00017.
Values sent between devices are 32-bit elements; how exact they have to be, the bound alone decides.
A program may use at most 64 MiB of HBM per device.

```python
import math
import jax
import jax.numpy as jnp
from jax import lax

MEMBERS = 256
ROWS = 512
OBS = 16384
PARAMS = 131072


def touch_ends(result, stream_key, low, high):
    spot = [jax.random.randint(jax.random.fold_in(stream_key, axis), (), 0, length) for axis, length in enumerate(result.shape)]
    widest = result.shape.index(max(result.shape))
    neighbour = spot[:widest] + [(spot[widest] + 1) % result.shape[widest]] + spot[widest + 1:]
    return result.at[tuple(spot)].set(low).at[tuple(neighbour)].set(high)


def spiked(result, rng, source, target, parts, factor):
    def block_of(position):
        return (jnp.arange(result.shape[position]) // (result.shape[position] // parts)).reshape((-1,) + (1,) * (result.ndim - 1 - position))

    near = jax.random.permutation(rng, parts)[block_of(target)]
    other_side = (block_of(target) + parts // 2) % parts
    return jnp.where((block_of(source) == near) | (block_of(source) == other_side), factor * result, result)


def block_levels(key, shape, split, smallest, top_value):
    def one(axis_at, shards_of):
        draws = jax.random.uniform(jax.random.fold_in(jax.random.fold_in(key, 6), axis_at), (shards_of,), jnp.float32, smallest / len(split), top_value / len(split))
        return jnp.repeat(jnp.exp(draws), shape[axis_at] // shards_of).reshape((-1,) + (1,) * (len(shape) - axis_at - 1))

    factor_of = one(*split[0])
    for cut in split[1:]:
        factor_of = factor_of * one(*cut)
    return factor_of


def normal_values(rng, dims, scale, bound, cuts=(), kind=jnp.bfloat16):
    entries = scale * jax.random.normal(rng, dims, jnp.float32)
    if cuts:
        entries = entries * block_levels(rng, dims, cuts, -0.22, 0.18)
    return jnp.clip(entries, -bound, bound).astype(kind)


def heavy_noise(key, extent, scale, reach, pieces, heavy, held_as=jnp.bfloat16):
    values = scale * jax.random.normal(key, extent, jnp.float32)
    if pieces:
        values = values * block_levels(key, extent, pieces, -0.22, 0.18)
    return jnp.clip(spiked(values, jax.random.fold_in(key, 3), *heavy), -reach, reach).astype(held_as)


def setup_inputs(seed: int = 0) -> dict:
    keys = jax.random.split(jax.random.key(seed), 7)
    return {
        "operator": heavy_noise(keys[0], (PARAMS, ROWS), PARAMS ** -0.5, 0.046875, ((0, 64),), (0, 1, 64, 4.0), jnp.float32),
        "ensemble": normal_values(keys[1], (MEMBERS, PARAMS), 1.0, 6.0, ((0, 8), (1, 64)), jnp.float32),
        "noise": normal_values(keys[2], (MEMBERS, ROWS), 1.0, 6.0, ((0, 8),), jnp.float32),
        "observations": normal_values(keys[3], (OBS,), 1.0, 6.0, (), jnp.float32),
        "variances": jnp.clip(jnp.exp(jax.random.uniform(keys[4], (OBS,), jnp.float32, math.log(0.25), math.log(4.0))), 0.25, 4.0),
        "rows": touch_ends(jax.random.randint(keys[5], (ROWS,), 0, OBS), jax.random.fold_in(keys[5], 1), 0, OBS - 1).astype(jnp.int32),
    }


def cholesky_solve(matrix, right):
    factor = jnp.linalg.cholesky(matrix)
    inner = lax.linalg.triangular_solve(factor, right, left_side=True, lower=True)
    return lax.linalg.triangular_solve(factor, inner, left_side=True, lower=True, transpose_a=True)

def reference(operator, ensemble, noise, observations, variances, rows):
    highest = lax.Precision.HIGHEST
    forward = jnp.dot(ensemble.astype(jnp.float32), operator.astype(jnp.float32), precision=highest, preferred_element_type=jnp.float32)
    obs_rows = jnp.take(observations, rows)
    var_rows = jnp.take(variances, rows)
    residual = obs_rows[None, :] + jnp.sqrt(var_rows)[None, :] * noise - forward
    spread = forward - lax.optimization_barrier(jnp.mean(forward, axis=0, keepdims=True))
    weighted = spread / var_rows[None, :]
    count = forward.shape[0]
    gram = jnp.dot(weighted.astype(jnp.float32), spread.T.astype(jnp.float32), precision=highest, preferred_element_type=jnp.float32)
    gram = gram + (count - 1) * jnp.eye(count, dtype=jnp.float32)
    cross = jnp.dot(weighted.astype(jnp.float32), residual.T.astype(jnp.float32), precision=highest, preferred_element_type=jnp.float32)
    weights = cholesky_solve(gram, cross)
    deviation = ensemble - lax.optimization_barrier(jnp.mean(ensemble, axis=0, keepdims=True))
    return ensemble + jnp.dot(weights.T.astype(jnp.float32), deviation.astype(jnp.float32), precision=highest, preferred_element_type=jnp.float32)
```

```python
import functools

import jax
import jax.numpy as jnp
from jax import lax
from jax.experimental import pallas as pl
from jax.experimental.pallas import tpu as pltpu
from jax.sharding import PartitionSpec as P

MESH = pl.DeviceIdType.MESH
CHUNKS = 8
F32 = jnp.float32
BF16 = jnp.bfloat16


def split(a):
    hi = a.astype(BF16)
    return hi, (a - hi.astype(F32)).astype(BF16)


def dot(a, b):
    return jnp.dot(a, b, preferred_element_type=F32)


def exchange_kernel(
    op_hbm, ens_hbm, fwd_all, ens_all,
    op_v, ens_v, zsrc, zrecv, ysrc, yrecv, fz,
    op_sem, ens_sem, own_sem,
    zs_sem, zr_sem, ys_sem, yr_sem, gs_sem, gr_sem,
    xs_sem, xr_sem, cs_sem, cr_sem,
    es_sem, er_sem, fs_sem, fr_sem,
):
    mem = lax.axis_index("mem")
    par = lax.axis_index("par")
    x, core = mem // 2, mem % 2
    y, z = par // 8, par % 8
    own = ens_hbm.shape[0]
    depth = op_hbm.shape[0] // CHUNKS
    twin = x * 2 + (1 - core)

    def at_z(d):
        return (mem, y * 8 + (z + d) % 8)

    def at_y(d):
        return (mem, ((y + d) % 8) * 8 + z)

    def mem_at(d):
        return ((x + d) % 4) * 2 + core

    ens_copy = pltpu.make_async_copy(ens_hbm, ens_v, ens_sem)
    ens_copy.start()
    op_copies = []
    for c in range(CHUNKS):
        rows = pl.ds(c * depth, depth)
        op_copies.append(pltpu.make_async_copy(op_hbm.at[rows], op_v.at[rows], op_sem.at[c]))
        op_copies[-1].start()

    barrier = pltpu.get_barrier_semaphore()
    friends = [at_z(d) for d in range(1, 8)] + [at_y(d) for d in range(1, 8)]
    friends += [(mem_at(d), par) for d in range(1, 4)] + [(twin, par)]
    for friend in friends:
        pl.semaphore_signal(barrier, inc=1, device_id=friend, device_id_type=MESH)
    pl.semaphore_wait(barrier, len(friends))

    def remote(src, dst, send, recv, device):
        copy = pltpu.make_async_remote_copy(
            src_ref=src, dst_ref=dst, send_sem=send, recv_sem=recv, device_id=device, device_id_type=MESH
        )
        copy.start()
        return copy

    own_rows = pl.ds(pl.multiple_of(mem * own, own), own)
    ens_out = [
        remote(ens_hbm, ens_all.at[own_rows], es_sem.at[d], er_sem.at[d], (mem_at(d), par)) for d in range(1, 4)
    ]
    twin_out = [remote(ens_hbm, ens_all.at[own_rows], fs_sem.at[0], fr_sem.at[0], (twin, par))]

    ens_copy.wait()
    own_copy = pltpu.make_async_copy(ens_v, ens_all.at[own_rows], own_sem)
    own_copy.start()

    total = jnp.zeros((own, op_hbm.shape[1]), F32)
    for c in range(CHUNKS):
        op_copies[c].wait()
        op_hi, op_lo = split(op_v[pl.ds(c * depth, depth), :])
        ens_hi, ens_lo = split(ens_v[:, pl.ds(c * depth, depth)])
        total += dot(ens_hi, op_hi) + dot(ens_lo, op_hi) + dot(ens_hi, op_lo)
    for q in range(8):
        zsrc[q] = total[(q // 4) * 16 : (q // 4) * 16 + 16, (q % 4) * 128 : (q % 4) * 128 + 128]

    z_out = [
        remote(zsrc.at[(z + d) % 8], zrecv.at[d], zs_sem.at[d], zr_sem.at[d], at_z(d)) for d in range(1, 8)
    ]
    part = zsrc[z]
    for d in range(1, 8):
        z_out[d - 1].wait_recv()
        part += zrecv[d]
    ysrc[...] = part
    y_out = [remote(ysrc, yrecv.at[d], ys_sem.at[d], yr_sem.at[d], at_y(d)) for d in range(1, 8)]
    for d in range(1, 8):
        y_out[d - 1].wait_recv()
        part += yrecv[d]
    fz[z] = part
    g_out = [remote(fz.at[z], fz.at[z], gs_sem.at[d], gr_sem.at[d], at_z(d)) for d in range(1, 8)]

    def forward_ens(d):
        ens_out[d - 1].wait_recv()
        rows = pl.ds(pl.multiple_of(((x + 4 - d) % 4) * 2 * own + core * own, own), own)
        twin_out.append(remote(ens_all.at[rows], ens_all.at[rows], fs_sem.at[d], fr_sem.at[d], (twin, par)))

    forward_ens(1)
    forward_ens(3)
    for d in range(1, 8):
        g_out[d - 1].wait_recv()
    x_out = [remote(fz, fwd_all.at[mem], xs_sem.at[d], xr_sem.at[d], (mem_at(d), par)) for d in range(1, 4)]
    c_out = [remote(fz, fwd_all.at[mem], cs_sem.at[0], cr_sem.at[0], (twin, par))]
    fwd_all[mem] = fz[...]
    forward_ens(2)
    for d in (1, 3, 2):
        x_out[d - 1].wait_recv()
        came = ((x + 4 - d) % 4) * 2 + core
        c_out.append(remote(fwd_all.at[came], fwd_all.at[came], cs_sem.at[d], cr_sem.at[d], (twin, par)))
    for copy in c_out + twin_out:
        copy.wait()
    for copy in z_out + y_out + g_out + ens_out + x_out:
        copy.wait_send()
    own_copy.wait()


def exchange(operator, ensemble):
    own, params = ensemble.shape
    rows = operator.shape[1]
    any_spec = pl.BlockSpec(memory_space=pl.ANY)
    dma = pltpu.SemaphoreType.DMA
    return pl.pallas_call(
        exchange_kernel,
        name="exchange",
        out_shape=(
            jax.ShapeDtypeStruct((8, 8, 16, 128), F32),
            jax.ShapeDtypeStruct((8 * own, params), F32),
        ),
        in_specs=[any_spec, any_spec],
        out_specs=(pl.BlockSpec(memory_space=pltpu.VMEM), any_spec),
        scratch_shapes=[
            pltpu.VMEM((params, rows), F32),
            pltpu.VMEM((own, params), F32),
            pltpu.VMEM((8, 16, 128), F32),
            pltpu.VMEM((8, 16, 128), F32),
            pltpu.VMEM((16, 128), F32),
            pltpu.VMEM((8, 16, 128), F32),
            pltpu.VMEM((8, 16, 128), F32),
            dma((CHUNKS,)), dma, dma,
            dma((8,)), dma((8,)), dma((8,)), dma((8,)), dma((8,)), dma((8,)),
            dma((4,)), dma((4,)), dma((4,)), dma((4,)),
            dma((4,)), dma((4,)), dma((4,)), dma((4,)),
        ],
        compiler_params=pltpu.CompilerParams(collective_id=0, has_side_effects=True),
    )(operator, ensemble)


def cholesky_solve(matrix, right):
    factor = jnp.linalg.cholesky(matrix)
    inner = lax.linalg.triangular_solve(factor, right, left_side=True, lower=True)
    return lax.linalg.triangular_solve(factor, inner, left_side=True, lower=True, transpose_a=True)


def per_device(operator, ensemble, noise, observations, variances, rows):
    highest = lax.Precision.HIGHEST
    own_members = ensemble.shape[0]
    member_index = lax.axis_index("mem")
    obs_rows = jnp.take(observations, rows)
    var_rows = jnp.take(variances, rows)
    pieces, gathered = exchange(operator, ensemble)
    all_forward = pieces.reshape(8, 2, 4, 16, 128).transpose(0, 1, 3, 2, 4).reshape(256, 512)
    forward = lax.dynamic_slice_in_dim(all_forward, member_index * own_members, own_members, 0)
    residual = obs_rows[None, :] + jnp.sqrt(var_rows)[None, :] * noise - forward
    spread = all_forward - jnp.mean(all_forward, axis=0, keepdims=True)
    weighted = spread / var_rows[None, :]
    gram_part = jnp.dot(weighted, spread.T, precision=highest, preferred_element_type=jnp.float32)
    cross_part = jnp.dot(weighted, residual.T, precision=highest, preferred_element_type=jnp.float32)
    members = all_forward.shape[0]
    gram = gram_part + (members - 1) * jnp.eye(members, dtype=jnp.float32)
    weights = cholesky_solve(gram, cross_part)
    deviation = gathered - jnp.mean(gathered, axis=0, keepdims=True)
    change = jnp.dot(weights.T, deviation, precision=highest, preferred_element_type=jnp.float32)
    return ensemble + change


def solution(mesh):
    return jax.shard_map(
        per_device,
        mesh=mesh,
        in_specs=(P("par", None), P("mem", "par"), P("mem", None), P(), P(), P()),
        out_specs=P("mem", "par"),
        check_vma=False,
    )
```

```python
import jax
import jax.numpy as jnp
from jax import lax
from jax.experimental import pallas as pl
from jax.experimental.pallas import tpu as pltpu
from jax.sharding import PartitionSpec as P

MESH = pl.DeviceIdType.MESH
CHUNKS = 8
BLOCK = 32
FAR_FIRST = (4, 3, 5, 2, 6, 1, 7)
NEAR_FIRST = (1, 7, 2, 6, 3, 5, 4)
F32 = jnp.float32
BF16 = jnp.bfloat16


def split(a):
    hi = a.astype(BF16)
    return hi, (a - hi.astype(F32)).astype(BF16)


def dot(a, b):
    return jnp.dot(a, b, preferred_element_type=F32)


def dot_rows(a, b):
    return lax.dot_general(a, b, (((1,), (1,)), ((), ())), preferred_element_type=F32)


def picked(tables, rows):
    n = rows.shape[1]
    high, low = rows // 128, rows % 128
    hot = (lax.broadcasted_iota(jnp.int32, (128, n), 0) == high).astype(BF16)
    mask = lax.broadcasted_iota(jnp.int32, (128, n), 0) == low
    out = []
    for table in tables:
        t = table.T
        first = t.astype(BF16)
        t = t - first.astype(F32)
        second = t.astype(BF16)
        third = (t - second.astype(F32)).astype(BF16)
        lines = (dot(first, hot) + dot(second, hot)) + dot(third, hot)
        out.append(jnp.sum(jnp.where(mask, lines, 0.0), axis=0, keepdims=True))
    return out


def exchange_kernel(
    op_hbm, ens_hbm, obs_ref, var_ref, rows_ref, fwd_all, ens_all, picks,
    op_v, ens_v, zsrc, zrecv, ysrc, yrecv,
    op_sem, ens_sem, own_sem,
    zs_sem, zr_sem, ys_sem, yr_sem, gs_sem, gr_sem,
    xs_sem, xr_sem, cs_sem, cr_sem,
    es_sem, er_sem, fs_sem, fr_sem,
):
    mem = lax.axis_index("mem")
    par = lax.axis_index("par")
    x, core = mem // 2, mem % 2
    y, z = par // 8, par % 8
    own = ens_hbm.shape[0]
    depth = op_hbm.shape[0] // CHUNKS
    twin = x * 2 + (1 - core)

    def at_z(d):
        return (mem, y * 8 + (z + d) % 8)

    def at_y(d):
        return (mem, ((y + d) % 8) * 8 + z)

    def mem_at(d):
        return ((x + d) % 4) * 2 + core

    def remote(src, dst, send, recv, device):
        copy = pltpu.make_async_remote_copy(
            src_ref=src, dst_ref=dst, send_sem=send, recv_sem=recv, device_id=device, device_id_type=MESH
        )
        copy.start()
        return copy

    barrier = pltpu.get_barrier_semaphore()
    friends = [at_z(d) for d in FAR_FIRST] + [at_y(d) for d in FAR_FIRST]
    friends += [(mem_at(d), par) for d in (2, 1, 3)] + [(twin, par)]
    for friend in friends:
        pl.semaphore_signal(barrier, inc=1, device_id=friend, device_id_type=MESH)

    ens_copy = pltpu.make_async_copy(ens_hbm, ens_v, ens_sem)
    ens_copy.start()
    op_copies = []
    for c in range(CHUNKS):
        lines = pl.ds(c * depth, depth)
        op_copies.append(pltpu.make_async_copy(op_hbm.at[lines], op_v.at[lines], op_sem.at[c]))
        op_copies[-1].start()

    own_rows = pl.ds(pl.multiple_of(mem * own, own), own)
    ens_copy.wait()
    own_copy = pltpu.make_async_copy(ens_v, ens_all.at[own_rows], own_sem)
    own_copy.start()

    total = jnp.zeros((own, op_hbm.shape[1]), F32)
    for c in range(CHUNKS):
        op_copies[c].wait()
        op_hi, op_lo = split(op_v[pl.ds(c * depth, depth), :])
        ens_hi, ens_lo = split(ens_v[:, pl.ds(c * depth, depth)])
        total += dot(ens_hi, op_hi) + dot(ens_lo, op_hi) + dot(ens_hi, op_lo)
    for q in range(8):
        zsrc[q] = total[(q // 4) * 16 : (q // 4) * 16 + 16, (q % 4) * 128 : (q % 4) * 128 + 128]

    pl.semaphore_wait(barrier, len(friends))

    z_out = {
        d: remote(zsrc.at[(z + d) % 8], zrecv.at[d], zs_sem.at[d], zr_sem.at[d], at_z(d)) for d in FAR_FIRST
    }
    ens_out = {
        d: remote(ens_hbm, ens_all.at[own_rows], es_sem.at[d], er_sem.at[d], (mem_at(d), par)) for d in (2, 1, 3)
    }
    twin_out = [remote(ens_hbm, ens_all.at[own_rows], fs_sem.at[0], fr_sem.at[0], (twin, par))]

    obs_rows, var_rows = picked((obs_ref[...], var_ref[...]), rows_ref[...])
    picks[...] = jnp.concatenate([obs_rows, var_rows] + [var_rows] * 6, axis=0)

    part = zsrc[z]
    for d in NEAR_FIRST:
        z_out[d].wait_recv()
        part += zrecv[d]
    ysrc[...] = part
    y_out = {d: remote(ysrc, yrecv.at[d], ys_sem.at[d], yr_sem.at[d], at_y(d)) for d in FAR_FIRST}
    for d in NEAR_FIRST:
        y_out[d].wait_recv()
        part += yrecv[d]
    fwd_all[mem, z] = part
    g_out = {
        d: remote(fwd_all.at[mem, z], fwd_all.at[mem, z], gs_sem.at[d], gr_sem.at[d], at_z(d)) for d in FAR_FIRST
    }

    x_out, c_out = {}, []

    def spread_piece(d):
        piece = fwd_all.at[mem, (z + 8 - d) % 8]
        for e in (2, 1, 3):
            x_out[e, d] = remote(piece, piece, xs_sem.at[e, d], xr_sem.at[e, d], (mem_at(e), par))
        c_out.append(remote(piece, piece, cs_sem.at[0, d], cr_sem.at[0, d], (twin, par)))

    def forward_ens(d):
        ens_out[d].wait_recv()
        lines = pl.ds(pl.multiple_of(((x + 4 - d) % 4) * 2 * own + core * own, own), own)
        twin_out.append(remote(ens_all.at[lines], ens_all.at[lines], fs_sem.at[d], fr_sem.at[d], (twin, par)))

    spread_piece(0)
    for d in NEAR_FIRST:
        g_out[d].wait_recv()
        spread_piece(d)
    forward_ens(1)
    forward_ens(3)
    for d in (0,) + NEAR_FIRST:
        for e in (1, 3, 2):
            x_out[e, d].wait_recv()
            piece = fwd_all.at[((x + 4 - e) % 4) * 2 + core, (z + 8 - d) % 8]
            c_out.append(remote(piece, piece, cs_sem.at[e, d], cr_sem.at[e, d], (twin, par)))
    forward_ens(2)
    for copy in c_out + twin_out:
        copy.wait()
    for group in (z_out, y_out, g_out, ens_out, x_out):
        for copy in group.values():
            copy.wait_send()
    own_copy.wait()


def exchange(operator, ensemble, obs, var, rows):
    own, params = ensemble.shape
    width = operator.shape[1]
    any_spec = pl.BlockSpec(memory_space=pl.ANY)
    vmem_spec = pl.BlockSpec(memory_space=pltpu.VMEM)
    dma = pltpu.SemaphoreType.DMA
    return pl.pallas_call(
        exchange_kernel,
        name="exchange",
        out_shape=(
            jax.ShapeDtypeStruct((8, 8, 16, 128), F32),
            jax.ShapeDtypeStruct((8 * own, params), F32),
            jax.ShapeDtypeStruct((8, width), F32),
        ),
        in_specs=[any_spec, any_spec, vmem_spec, vmem_spec, vmem_spec],
        out_specs=(vmem_spec, any_spec, vmem_spec),
        scratch_shapes=[
            pltpu.VMEM((params, width), F32),
            pltpu.VMEM((own, params), F32),
            pltpu.VMEM((8, 16, 128), F32),
            pltpu.VMEM((8, 16, 128), F32),
            pltpu.VMEM((16, 128), F32),
            pltpu.VMEM((8, 16, 128), F32),
            dma((CHUNKS,)), dma, dma,
            dma((8,)), dma((8,)), dma((8,)), dma((8,)), dma((8,)), dma((8,)),
            dma((4, 8)), dma((4, 8)), dma((4, 8)), dma((4, 8)),
            dma((4,)), dma((4,)), dma((4,)), dma((4,)),
        ],
        compiler_params=pltpu.CompilerParams(collective_id=0, has_side_effects=True),
    )(operator, ensemble, obs, var, rows)


def row_of(tile, i):
    return jnp.broadcast_to(tile[i:i+1, :], (8, 128))


def factor(m_ref, size, block):
    lanes = size // 128
    tiles = block // 8
    sub = lax.broadcasted_iota(jnp.int32, (8, 128), 0)
    lane = lax.broadcasted_iota(jnp.int32, (8, 128), 1)
    for k in range(size // block):
        base = k * block
        home, shift = base // 128, base % 128
        square = [m_ref[base + 8 * t: base + 8 * t + 8, home * 128: home * 128 + 128] for t in range(tiles)]
        panel = []
        for t in range(tiles):
            line = []
            for l in range(lanes):
                v = m_ref[base + 8 * t: base + 8 * t + 8, l * 128: l * 128 + 128]
                if l == home:
                    inside = (lane >= shift) & (lane < shift + block)
                    v = jnp.where(inside, (lane - shift == sub + 8 * t).astype(F32), v)
                line.append(v)
            panel.append(line)
        done = [[None] * lanes for _ in range(tiles)]
        cols = []
        for j in range(block):
            first = j // 8
            col = [jnp.broadcast_to(square[t][:, shift + j: shift + j + 1], (8, 128)) for t in range(first, tiles)]
            for p in range(j):
                scale = row_of(cols[p][first - p // 8], j % 8)
                for t in range(first, tiles):
                    col[t - first] = col[t - first] - cols[p][t - p // 8] * scale
            inv = lax.rsqrt(row_of(col[0], j % 8))
            col = [c * inv for c in col]
            cols.append(col)
            below = jnp.where(sub > j % 8, col[0], 0.0)
            for l in range(lanes):
                line = row_of(panel[first][l], j % 8) * inv
                old = done[first][l]
                done[first][l] = line if old is None else jnp.where(sub >= j % 8, line, old)
                for t in range(first, tiles):
                    panel[t][l] = panel[t][l] - (below if t == first else col[t - first]) * line
        z = jnp.concatenate([jnp.concatenate(done[t], axis=1) for t in range(tiles)], axis=0)
        m_ref[base: base + block, :] = z
        after = base + block
        if after < size:
            hi, lo = split(z)
            left = jnp.concatenate([hi, hi, lo], axis=0).T
            right = jnp.concatenate([hi, lo, hi], axis=0)
            update = jnp.dot(left[after:], right, preferred_element_type=F32)
            rest = m_ref[after:, :]
            col_id = lax.broadcasted_iota(jnp.int32, rest.shape, 1)
            rest = jnp.where((col_id >= base) & (col_id < after), 0.0, rest)
            m_ref[after:, :] = rest - update


def dot3(a, b, product=dot):
    a_hi, a_lo = split(a)
    b_hi, b_lo = split(b)
    return product(a_hi, b_hi) + product(a_lo, b_hi) + product(a_hi, b_lo)


def update_kernel(fwd_ref, ens_all, ens_ref, noise_ref, picks_ref, out_ref, ens_v, m_ref, ens_sem):
    mem = lax.axis_index("mem")
    ens_copy = pltpu.make_async_copy(ens_all, ens_v, ens_sem)
    ens_copy.start()

    def rows_of(m):
        halves = [jnp.concatenate([fwd_ref[m, h * 4 + l] for l in range(4)], axis=1) for h in range(2)]
        return jnp.concatenate(halves, axis=0)

    forward = jnp.concatenate([rows_of(m) for m in range(8)], axis=0)
    members = forward.shape[0]
    obs_rows, var_rows = picks_ref[0:1, :], picks_ref[1:2, :]
    scale = lax.rsqrt(var_rows)
    spread = (forward - jnp.mean(forward, axis=0, keepdims=True)) * scale
    residual = (obs_rows + jnp.sqrt(var_rows) * noise_ref[...] - rows_of(mem)) * scale
    both = (members, members)
    eye = (lax.broadcasted_iota(jnp.int32, both, 0) == lax.broadcasted_iota(jnp.int32, both, 1)).astype(F32)
    m_ref[...] = dot3(spread, spread, dot_rows) + (members - 1) * eye
    factor(m_ref, members, BLOCK)
    cross = dot3(residual, spread, dot_rows)
    lower = lax.broadcasted_iota(jnp.int32, both, 0) >= lax.broadcasted_iota(jnp.int32, both, 1)
    inverse = jnp.where(lower, m_ref[...], 0.0)
    weights = dot3(dot3(cross, inverse, dot_rows), inverse)
    weights = weights - jnp.mean(weights, axis=1, keepdims=True)
    ens_copy.wait()
    step = 512
    for c in range(out_ref.shape[1] // step):
        part = pl.ds(c * step, step)
        out_ref[:, part] = ens_ref[:, part] + dot3(weights, ens_v[:, part])


def update(pieces, gathered, ensemble, noise, picks):
    vmem_spec = pl.BlockSpec(memory_space=pltpu.VMEM)
    return pl.pallas_call(
        update_kernel,
        name="update",
        out_shape=jax.ShapeDtypeStruct(ensemble.shape, F32),
        in_specs=[vmem_spec, pl.BlockSpec(memory_space=pl.ANY), vmem_spec, vmem_spec, vmem_spec],
        out_specs=vmem_spec,
        scratch_shapes=[
            pltpu.VMEM(gathered.shape, F32),
            pltpu.VMEM((gathered.shape[0],) * 2, F32),
            pltpu.SemaphoreType.DMA,
        ],
    )(pieces, gathered, ensemble, noise, picks)


def per_device(operator, ensemble, noise, observations, variances, rows):
    obs, var = observations.reshape(128, 128), variances.reshape(128, 128)
    pieces, gathered, picks = exchange(operator, ensemble, obs, var, rows.reshape(1, -1))
    return update(pieces, gathered, ensemble, noise, picks)


def solution(mesh):
    return jax.shard_map(
        per_device,
        mesh=mesh,
        in_specs=(P("par", None), P("mem", "par"), P("mem", None), P(), P(), P()),
        out_specs=P("mem", "par"),
        check_vma=False,
    )
```

```python
import jax
import jax.numpy as jnp
from jax import lax
from jax.experimental import pallas as pl
from jax.experimental.pallas import tpu as pltpu
from jax.sharding import PartitionSpec as P

MESH = pl.DeviceIdType.MESH
CHUNKS = 4
BLOCK = 32
FRONTS = {0: (0, 16), 12: (16, 32)}
FAR_FIRST = (4, 3, 5, 2, 6, 1, 7)
NEAR = (1, 7, 2, 6)
FAR = (4, 3, 5)
F32 = jnp.float32
BF16 = jnp.bfloat16


def split(a):
    hi = a.astype(BF16)
    return hi, (a - hi.astype(F32)).astype(BF16)


def dot(a, b):
    return jnp.dot(a, b, preferred_element_type=F32)


def dot_rows(a, b):
    return lax.dot_general(a, b, (((1,), (1,)), ((), ())), preferred_element_type=F32)


def picked(tables, rows):
    n = rows.shape[1]
    high, low = rows // 128, rows % 128
    hot = (lax.broadcasted_iota(jnp.int32, (128, n), 0) == high).astype(BF16)
    mask = lax.broadcasted_iota(jnp.int32, (128, n), 0) == low
    out = []
    for table in tables:
        t = table.T
        first = t.astype(BF16)
        t = t - first.astype(F32)
        second = t.astype(BF16)
        third = (t - second.astype(F32)).astype(BF16)
        lines = (dot(first, hot) + dot(second, hot)) + dot(third, hot)
        out.append(jnp.sum(jnp.where(mask, lines, 0.0), axis=0, keepdims=True))
    return out


def exchange_kernel(
    op_hbm, ens_hbm, obs_hbm, var_hbm, rows_hbm, fwd_all, ens_all, picks,
    op_v, ens_v, obs_v, var_v, rows_v, source, came_one, middle, came_two,
    op_sem, load_sem, own_sem, send_sem, one_r, two_r, three_r, x_r, twin_r, ens_r, ens_twin_r,
):
    mem = lax.axis_index("mem")
    par = lax.axis_index("par")
    x, core = mem // 2, mem % 2
    y, z = par // 8, par % 8
    own = ens_hbm.shape[0]
    depth = op_hbm.shape[0] // CHUNKS
    twin = x * 2 + (1 - core)

    def at_z(d):
        return (mem, y * 8 + (z + d) % 8)

    def at_y(d):
        return (mem, ((y + d) % 8) * 8 + z)

    def mem_at(d):
        return ((x + d) % 4) * 2 + core

    across, along, place = (at_z, at_y), (at_y, at_z), (z, y)

    def copy_to(src, dst, send, recv, device):
        return pltpu.make_async_remote_copy(
            src_ref=src, dst_ref=dst, send_sem=send, recv_sem=recv, device_id=device, device_id_type=MESH
        )

    def arrived(ref, recv):
        copy_to(ref, ref, send_sem.at[0], recv, (twin, par)).wait_recv()

    def sent(ref, send):
        copy_to(ref, ref, send, one_r.at[0], (twin, par)).wait_send()

    barrier = pltpu.get_barrier_semaphore()
    friends = [at(d) for d in FAR_FIRST for at in across]
    friends += [(mem_at(d), par) for d in (2, 1, 3)] + [(twin, par)]
    for friend in friends:
        pl.semaphore_signal(barrier, inc=1, device_id=friend, device_id_type=MESH)

    ens_copy = pltpu.make_async_copy(ens_hbm, ens_v, load_sem.at[0])
    ens_copy.start()
    op_copies = []
    for c in range(CHUNKS):
        lines = pl.ds(c * depth, depth)
        op_copies.append(pltpu.make_async_copy(op_hbm.at[lines], op_v.at[lines], op_sem.at[c]))
        op_copies[-1].start()
    small = [
        pltpu.make_async_copy(src, dst, load_sem.at[i])
        for i, src, dst in ((1, obs_hbm, obs_v), (2, var_hbm, var_v), (3, rows_hbm, rows_v))
    ]
    for copy in small:
        copy.start()

    own_rows = pl.ds(pl.multiple_of(mem * own, own), own)
    ens_copy.wait()
    own_copy = pltpu.make_async_copy(ens_v, ens_all.at[own_rows], own_sem)
    own_copy.start()

    total = jnp.zeros((own, op_hbm.shape[1]), F32)
    for c in range(CHUNKS):
        op_copies[c].wait()
        op_hi, op_lo = split(op_v[pl.ds(c * depth, depth), :])
        ens_hi, ens_lo = split(ens_v[:, pl.ds(c * depth, depth)])
        total += dot(ens_hi, op_hi) + dot(ens_lo, op_hi) + dot(ens_hi, op_lo)
    for h in range(2):
        for q in range(8):
            top, left = (q // 2) * 8, h * 256 + (q % 2) * 128
            source[h, q] = total[top : top + 8, left : left + 128]

    pl.semaphore_wait(barrier, len(friends))

    for d in FAR_FIRST:
        for h in range(2):
            piece = source.at[h, (place[h] + d) % 8]
            copy_to(piece, came_one.at[h, d], send_sem.at[0], one_r.at[h], across[h](d)).start()
    for d in (1, 3):
        copy_to(ens_hbm, ens_all.at[own_rows], send_sem.at[3], ens_r.at[d], (mem_at(d), par)).start()
    copy_to(ens_hbm, ens_all.at[own_rows], send_sem.at[4], ens_twin_r, (twin, par)).start()

    for copy in small:
        copy.wait()
    obs_rows, var_rows = picked((obs_v[...], var_v[...]), rows_v[...])
    picks[...] = jnp.concatenate([obs_rows, var_rows] + [var_rows] * 6, axis=0)

    others = pl.ds(1, 7)
    part = [None, None]
    for h in range(2):
        arrived(came_one.at[h, others], one_r.at[h])
        part[h] = source[h, place[h]]
        for d in range(1, 8):
            part[h] += came_one[h, d]
        middle[h] = part[h]
        for d in FAR_FIRST:
            copy_to(middle.at[h], came_two.at[h, d], send_sem.at[1], two_r.at[h], along[h](d)).start()
    for h in range(2):
        arrived(came_two.at[h, others], two_r.at[h])
        for d in range(1, 8):
            part[h] += came_two[h, d]
        fwd_all[mem, h, place[h]] = part[h]
        piece = fwd_all.at[mem, h, place[h]]
        for d in FAR_FIRST:
            copy_to(piece, piece, send_sem.at[2], three_r.at[int(d in FAR), h], across[h](d)).start()

    def spread_piece(h, d):
        piece = fwd_all.at[mem, h, (place[h] + 8 - d) % 8]
        for e in (2, 1, 3):
            copy_to(piece, piece, send_sem.at[5], x_r.at[int(d in FAR)], (mem_at(e), par)).start()
        copy_to(piece, piece, send_sem.at[6], twin_r, (twin, par)).start()

    def ens_rows(d, first, count):
        return pl.ds(pl.multiple_of(((x + 4 - d) % 4) * 2 * own + core * own + first, count), count)

    def ens_to_twin(lines):
        copy_to(ens_all.at[lines], ens_all.at[lines], send_sem.at[4], ens_twin_r, (twin, par)).start()

    half = own // 2
    for h in range(2):
        spread_piece(h, 0)
    for i, d in ((0, 1), (1, 3)):
        arrived(ens_all.at[ens_rows(d, 0, own)], ens_r.at[d])
        lines = ens_rows(d, i * half, half)
        copy_to(ens_all.at[lines], ens_all.at[lines], send_sem.at[3], ens_r.at[2 * i], (mem_at(d), par)).start()
        ens_to_twin(ens_rows(d, 0, own))
    for far, group in enumerate((NEAR, FAR)):
        for h in range(2):
            arrived(fwd_all.at[mem, h, pl.ds(0, len(group))], three_r.at[far, h])
            for d in group:
                spread_piece(h, d)
    for i in range(2):
        lines = ens_rows(2, i * half, half)
        arrived(ens_all.at[lines], ens_r.at[2 * i])
        ens_to_twin(lines)
    for far, group in enumerate(((0,) + NEAR, FAR)):
        arrived(fwd_all.at[pl.ds(0, 3), :, pl.ds(0, len(group))], x_r.at[far])
        for d in group:
            for h in range(2):
                for e in (1, 3, 2):
                    piece = fwd_all.at[((x + 4 - e) % 4) * 2 + core, h, (place[h] + 8 - d) % 8]
                    copy_to(piece, piece, send_sem.at[6], twin_r, (twin, par)).start()
    arrived(fwd_all.at[pl.ds(0, 4)], twin_r)
    arrived(ens_all.at[pl.ds(0, 4 * own)], ens_twin_r)
    for i in range(2):
        sent(came_one.at[:, others], send_sem.at[i])
    sent(came_one.at[:, others], send_sem.at[2])
    sent(ens_all.at[pl.ds(0, 3 * own)], send_sem.at[3])
    sent(ens_all.at[pl.ds(0, 4 * own)], send_sem.at[4])
    sent(fwd_all.at[pl.ds(0, 3)], send_sem.at[5])
    sent(fwd_all.at[pl.ds(0, 4)], send_sem.at[6])
    own_copy.wait()


def exchange(operator, ensemble, obs, var, rows):
    own, params = ensemble.shape
    width = operator.shape[1]
    any_spec = pl.BlockSpec(memory_space=pl.ANY)
    vmem_spec = pl.BlockSpec(memory_space=pltpu.VMEM)
    dma = pltpu.SemaphoreType.DMA
    return pl.pallas_call(
        exchange_kernel,
        name="exchange",
        out_shape=(
            jax.ShapeDtypeStruct((8, 2, 8, 8, 128), F32),
            jax.ShapeDtypeStruct((8 * own, params), F32),
            jax.ShapeDtypeStruct((8, width), F32),
        ),
        in_specs=[any_spec] * 5,
        out_specs=(vmem_spec, any_spec, vmem_spec),
        scratch_shapes=[
            pltpu.VMEM((params, width), F32),
            pltpu.VMEM((own, params), F32),
            pltpu.VMEM(obs.shape, F32),
            pltpu.VMEM(var.shape, F32),
            pltpu.VMEM(rows.shape, rows.dtype),
            pltpu.VMEM((2, 8, 8, 128), F32),
            pltpu.VMEM((2, 8, 8, 128), F32),
            pltpu.VMEM((2, 8, 128), F32),
            pltpu.VMEM((2, 8, 8, 128), F32),
            dma((CHUNKS,)), dma((4,)), dma, dma((7,)),
            dma((2,)), dma((2,)), dma((2, 2)), dma((2,)), dma, dma((4,)), dma,
        ],
        compiler_params=pltpu.CompilerParams(collective_id=0, has_side_effects=True),
    )(operator, ensemble, obs, var, rows)


def row_of(tile, i):
    return jnp.broadcast_to(tile[i:i+1, :], (8, 128))


def factor(m_ref, size, block):
    lanes = size // 128
    tiles = block // 8
    sub = lax.broadcasted_iota(jnp.int32, (8, 128), 0)
    lane = lax.broadcasted_iota(jnp.int32, (8, 128), 1)
    for k in range(size // block):
        base = k * block
        home, shift = base // 128, base % 128
        panel = []
        for t in range(tiles):
            line = [m_ref[base + 8 * t: base + 8 * t + 8, l * 128: l * 128 + 128] for l in range(lanes)]
            line.append(line[home])
            inside = (lane >= shift) & (lane < shift + block)
            line[home] = jnp.where(inside, (lane - shift == sub + 8 * t).astype(F32), line[home])
            panel.append(line)
        done = [[None] * lanes for _ in range(tiles)]
        cols, raw, invs, fronts, seen = [], [], [], {}, {}
        for j in range(block):
            if j in FRONTS:
                lo_c, hi_c = FRONTS[j]
                for c in range(lo_c, hi_c):
                    fronts[c] = [jnp.broadcast_to(panel[t][lanes][:, shift + c: shift + c + 1], (8, 128)) for t in range(c // 8, tiles)]
                    seen[c] = j
            first = j // 8
            col = fronts[j]
            for p in range(seen[j], j):
                if p == j - 1:
                    scale = row_of(raw[p][first - p // 8], j % 8)
                    for t in range(first, tiles):
                        col[t - first] = col[t - first] - raw[p][t - p // 8] * scale * invs[p]
                else:
                    scale = row_of(cols[p][first - p // 8], j % 8)
                    for t in range(first, tiles):
                        col[t - first] = col[t - first] - cols[p][t - p // 8] * scale
            raw.append(col)
            pivot = row_of(col[0], j % 8)
            invs.append(1.0 / pivot)
            inv = lax.rsqrt(pivot)
            col = [c * inv for c in col]
            cols.append(col)
            below = jnp.where(sub > j % 8, col[0], 0.0)
            for l in range(lanes + 1 if j < max(FRONTS) else lanes):
                line = row_of(panel[first][l], j % 8) * inv
                if l < lanes:
                    old = done[first][l]
                    done[first][l] = line if old is None else jnp.where(sub >= j % 8, line, old)
                for t in range(first, tiles):
                    panel[t][l] = panel[t][l] - (below if t == first else col[t - first]) * line
        z = jnp.concatenate([jnp.concatenate(done[t], axis=1) for t in range(tiles)], axis=0)
        m_ref[base: base + block, :] = z
        after = base + block
        if after < size:
            hi, lo = split(z)
            left = jnp.concatenate([hi, hi, lo], axis=0).T
            right = jnp.concatenate([hi, lo, hi], axis=0)
            update = jnp.dot(left[after:], right, preferred_element_type=F32)
            rest = m_ref[after:, :]
            col_id = lax.broadcasted_iota(jnp.int32, rest.shape, 1)
            rest = jnp.where((col_id >= base) & (col_id < after), 0.0, rest)
            m_ref[after:, :] = rest - update


def dot3(a, b, product=dot):
    a_hi, a_lo = split(a)
    b_hi, b_lo = split(b)
    return product(a_hi, b_hi) + product(a_lo, b_hi) + product(a_hi, b_lo)


def update_kernel(fwd_ref, ens_all, ens_ref, noise_ref, picks_ref, out_ref, ens_v, m_ref, ens_sem):
    mem = lax.axis_index("mem")
    ens_copy = pltpu.make_async_copy(ens_all, ens_v, ens_sem)
    ens_copy.start()

    def rows_of(m):
        lines = [[fwd_ref[m, h, r * 2 + l] for h in range(2) for l in range(2)] for r in range(4)]
        return jnp.concatenate([jnp.concatenate(line, axis=1) for line in lines], axis=0)

    forward = jnp.concatenate([rows_of(m) for m in range(8)], axis=0)
    members = forward.shape[0]
    obs_rows, var_rows = picks_ref[0:1, :], picks_ref[1:2, :]
    scale = lax.rsqrt(var_rows)
    spread = (forward - jnp.mean(forward, axis=0, keepdims=True)) * scale
    residual = (obs_rows + jnp.sqrt(var_rows) * noise_ref[...] - rows_of(mem)) * scale
    both = (members, members)
    eye = (lax.broadcasted_iota(jnp.int32, both, 0) == lax.broadcasted_iota(jnp.int32, both, 1)).astype(F32)
    m_ref[...] = dot3(spread, spread, dot_rows) + (members - 1) * eye
    factor(m_ref, members, BLOCK)
    cross = dot3(residual, spread, dot_rows)
    lower = lax.broadcasted_iota(jnp.int32, both, 0) >= lax.broadcasted_iota(jnp.int32, both, 1)
    inverse = jnp.where(lower, m_ref[...], 0.0)
    weights = dot3(dot3(cross, inverse, dot_rows), inverse)
    weights = weights - jnp.mean(weights, axis=1, keepdims=True)
    ens_copy.wait()
    step = 512
    for c in range(out_ref.shape[1] // step):
        part = pl.ds(c * step, step)
        out_ref[:, part] = ens_ref[:, part] + dot3(weights, ens_v[:, part])


def update(pieces, gathered, ensemble, noise, picks):
    vmem_spec = pl.BlockSpec(memory_space=pltpu.VMEM)
    return pl.pallas_call(
        update_kernel,
        name="update",
        out_shape=jax.ShapeDtypeStruct(ensemble.shape, F32),
        in_specs=[vmem_spec, pl.BlockSpec(memory_space=pl.ANY), vmem_spec, vmem_spec, vmem_spec],
        out_specs=vmem_spec,
        scratch_shapes=[
            pltpu.VMEM(gathered.shape, F32),
            pltpu.VMEM((gathered.shape[0],) * 2, F32),
            pltpu.SemaphoreType.DMA,
        ],
    )(pieces, gathered, ensemble, noise, picks)


def per_device(operator, ensemble, noise, observations, variances, rows):
    obs, var = observations.reshape(128, 128), variances.reshape(128, 128)
    pieces, gathered, picks = exchange(operator, ensemble, obs, var, rows.reshape(1, -1))
    return update(pieces, gathered, ensemble, noise, picks)


def solution(mesh):
    return jax.shard_map(
        per_device,
        mesh=mesh,
        in_specs=(P("par", None), P("mem", "par"), P("mem", None), P(), P(), P()),
        out_specs=P("mem", "par"),
        check_vma=False,
    )
```

```python
import jax
import jax.numpy as jnp
from jax import lax
from jax.experimental import pallas as pl
from jax.experimental.pallas import tpu as pltpu
from jax.sharding import PartitionSpec as P

MESH = pl.DeviceIdType.MESH
CHUNKS = 4
BLOCK = 32
FRONTS = {0: (0, 16), 12: (16, 32)}
FAR_FIRST = (4, 3, 5, 2, 6, 1, 7)
NEAR = (1, 7, 2, 6)
FAR = (4, 3, 5)
F32 = jnp.float32
BF16 = jnp.bfloat16


def split(a):
    hi = a.astype(BF16)
    return hi, (a - hi.astype(F32)).astype(BF16)


def dot(a, b):
    return jnp.dot(a, b, preferred_element_type=F32)


def dot_rows(a, b):
    return lax.dot_general(a, b, (((1,), (1,)), ((), ())), preferred_element_type=F32)


def picked(tables, rows):
    n = rows.shape[1]
    high, low = rows // 128, rows % 128
    hot = (lax.broadcasted_iota(jnp.int32, (128, n), 0) == high).astype(BF16)
    mask = lax.broadcasted_iota(jnp.int32, (128, n), 0) == low
    out = []
    for table in tables:
        t = table.T
        first = t.astype(BF16)
        t = t - first.astype(F32)
        second = t.astype(BF16)
        third = (t - second.astype(F32)).astype(BF16)
        lines = (dot(first, hot) + dot(second, hot)) + dot(third, hot)
        out.append(jnp.sum(jnp.where(mask, lines, 0.0), axis=0, keepdims=True))
    return out


def exchange_kernel(
    op_hbm, ens_hbm, obs_hbm, var_hbm, rows_hbm, fwd_all, ens_all, picks,
    op_v, obs_v, var_v, rows_v, source, came_one, middle, came_two,
    op_sem, load_sem, send_sem, one_r, two_r, three_r, x_r, twin_r, ens_r, ens_twin_r,
):
    mem = lax.axis_index("mem")
    par = lax.axis_index("par")
    x, core = mem // 2, mem % 2
    y, z = par // 8, par % 8
    own = ens_hbm.shape[0]
    depth = op_hbm.shape[0] // CHUNKS
    twin = x * 2 + (1 - core)

    def at_z(d):
        return (mem, y * 8 + (z + d) % 8)

    def at_y(d):
        return (mem, ((y + d) % 8) * 8 + z)

    def mem_at(d):
        return ((x + d) % 4) * 2 + core

    across, along, place = (at_z, at_y), (at_y, at_z), (z, y)

    def copy_to(src, dst, send, recv, device):
        return pltpu.make_async_remote_copy(
            src_ref=src, dst_ref=dst, send_sem=send, recv_sem=recv, device_id=device, device_id_type=MESH
        )

    def arrived(ref, recv):
        copy_to(ref, ref, send_sem.at[0], recv, (twin, par)).wait_recv()

    def sent(ref, send):
        copy_to(ref, ref, send, one_r.at[0], (twin, par)).wait_send()

    barrier = pltpu.get_barrier_semaphore()
    friends = [at(d) for d in FAR_FIRST for at in across]
    friends += [(mem_at(d), par) for d in (2, 1, 3)] + [(twin, par)]
    for friend in friends:
        pl.semaphore_signal(barrier, inc=1, device_id=friend, device_id_type=MESH)

    own_rows = pl.ds(pl.multiple_of(mem * own, own), own)
    own_ens = ens_all.at[own_rows]
    ens_copy = pltpu.make_async_copy(ens_hbm, own_ens, load_sem.at[0])
    ens_copy.start()
    op_copies = []
    for c in range(CHUNKS):
        lines = pl.ds(c * depth, depth)
        op_copies.append(pltpu.make_async_copy(op_hbm.at[lines], op_v.at[lines], op_sem.at[c]))
        op_copies[-1].start()
    small = [
        pltpu.make_async_copy(src, dst, load_sem.at[i])
        for i, src, dst in ((1, obs_hbm, obs_v), (2, var_hbm, var_v), (3, rows_hbm, rows_v))
    ]
    for copy in small:
        copy.start()

    ens_copy.wait()

    total = jnp.zeros((own, op_hbm.shape[1]), F32)
    for c in range(CHUNKS):
        op_copies[c].wait()
        op_hi, op_lo = split(op_v[pl.ds(c * depth, depth), :])
        ens_hi, ens_lo = split(ens_all[own_rows, pl.ds(c * depth, depth)])
        total += dot(ens_hi, op_hi) + dot(ens_lo, op_hi) + dot(ens_hi, op_lo)
    for h in range(2):
        for q in range(8):
            top, left = (q // 2) * 8, h * 256 + (q % 2) * 128
            source[h, q] = total[top : top + 8, left : left + 128]

    pl.semaphore_wait(barrier, len(friends))

    for d in FAR_FIRST:
        for h in range(2):
            piece = source.at[h, (place[h] + d) % 8]
            copy_to(piece, came_one.at[h, d], send_sem.at[0], one_r.at[h], across[h](d)).start()
    for d in (1, 3):
        copy_to(own_ens, own_ens, send_sem.at[3], ens_r.at[d], (mem_at(d), par)).start()
    copy_to(own_ens, own_ens, send_sem.at[4], ens_twin_r, (twin, par)).start()

    for copy in small:
        copy.wait()
    obs_rows, var_rows = picked((obs_v[...], var_v[...]), rows_v[...])
    picks[...] = jnp.concatenate([obs_rows, var_rows] + [var_rows] * 6, axis=0)

    others = pl.ds(1, 7)
    part = [None, None]
    for h in range(2):
        arrived(came_one.at[h, others], one_r.at[h])
        part[h] = source[h, place[h]]
        for d in range(1, 8):
            part[h] += came_one[h, d]
        middle[h] = part[h]
        for d in FAR_FIRST:
            copy_to(middle.at[h], came_two.at[h, d], send_sem.at[1], two_r.at[h], along[h](d)).start()
    for h in range(2):
        arrived(came_two.at[h, others], two_r.at[h])
        for d in range(1, 8):
            part[h] += came_two[h, d]
        fwd_all[mem, h, place[h]] = part[h]
        piece = fwd_all.at[mem, h, place[h]]
        for d in FAR_FIRST:
            copy_to(piece, piece, send_sem.at[2], three_r.at[int(d in FAR), h], across[h](d)).start()

    def spread_piece(h, d):
        piece = fwd_all.at[mem, h, (place[h] + 8 - d) % 8]
        for e in (2, 1, 3):
            copy_to(piece, piece, send_sem.at[5], x_r.at[int(d in FAR)], (mem_at(e), par)).start()
        copy_to(piece, piece, send_sem.at[6], twin_r, (twin, par)).start()

    def ens_rows(d, first, count):
        return pl.ds(pl.multiple_of(((x + 4 - d) % 4) * 2 * own + core * own + first, count), count)

    def ens_to_twin(lines):
        copy_to(ens_all.at[lines], ens_all.at[lines], send_sem.at[4], ens_twin_r, (twin, par)).start()

    half = own // 2
    for h in range(2):
        spread_piece(h, 0)
    for i, d in ((0, 1), (1, 3)):
        arrived(ens_all.at[ens_rows(d, 0, own)], ens_r.at[d])
        lines = ens_rows(d, i * half, half)
        copy_to(ens_all.at[lines], ens_all.at[lines], send_sem.at[3], ens_r.at[2 * i], (mem_at(d), par)).start()
        ens_to_twin(ens_rows(d, 0, own))
    for far, group in enumerate((NEAR, FAR)):
        for h in range(2):
            arrived(fwd_all.at[mem, h, pl.ds(0, len(group))], three_r.at[far, h])
            for d in group:
                spread_piece(h, d)
    for i in range(2):
        lines = ens_rows(2, i * half, half)
        arrived(ens_all.at[lines], ens_r.at[2 * i])
        ens_to_twin(lines)
    for far, group in enumerate(((0,) + NEAR, FAR)):
        arrived(fwd_all.at[pl.ds(0, 3), :, pl.ds(0, len(group))], x_r.at[far])
        for d in group:
            for h in range(2):
                for e in (1, 3, 2):
                    piece = fwd_all.at[((x + 4 - e) % 4) * 2 + core, h, (place[h] + 8 - d) % 8]
                    copy_to(piece, piece, send_sem.at[6], twin_r, (twin, par)).start()
    arrived(fwd_all.at[pl.ds(0, 4)], twin_r)
    arrived(ens_all.at[pl.ds(0, 4 * own)], ens_twin_r)
    for i in range(2):
        sent(came_one.at[:, others], send_sem.at[i])
    sent(came_one.at[:, others], send_sem.at[2])
    sent(ens_all.at[pl.ds(0, 3 * own)], send_sem.at[3])
    sent(ens_all.at[pl.ds(0, 4 * own)], send_sem.at[4])
    sent(fwd_all.at[pl.ds(0, 3)], send_sem.at[5])
    sent(fwd_all.at[pl.ds(0, 4)], send_sem.at[6])


def exchange(operator, ensemble, obs, var, rows):
    own, params = ensemble.shape
    width = operator.shape[1]
    any_spec = pl.BlockSpec(memory_space=pl.ANY)
    vmem_spec = pl.BlockSpec(memory_space=pltpu.VMEM)
    dma = pltpu.SemaphoreType.DMA
    return pl.pallas_call(
        exchange_kernel,
        name="exchange",
        out_shape=(
            pltpu.VMEM((8, 2, 8, 8, 128), F32),
            pltpu.VMEM((8 * own, params), F32),
            pltpu.VMEM((8, width), F32),
        ),
        in_specs=[any_spec] * 5,
        out_specs=(vmem_spec,) * 3,
        scratch_shapes=[
            pltpu.VMEM((params, width), F32),
            pltpu.VMEM(obs.shape, F32),
            pltpu.VMEM(var.shape, F32),
            pltpu.VMEM(rows.shape, rows.dtype),
            pltpu.VMEM((2, 8, 8, 128), F32),
            pltpu.VMEM((2, 8, 8, 128), F32),
            pltpu.VMEM((2, 8, 128), F32),
            pltpu.VMEM((2, 8, 8, 128), F32),
            dma((CHUNKS,)), dma((4,)), dma((7,)),
            dma((2,)), dma((2,)), dma((2, 2)), dma((2,)), dma, dma((4,)), dma,
        ],
        compiler_params=pltpu.CompilerParams(collective_id=0, has_side_effects=True),
    )(operator, ensemble, obs, var, rows)


def row_of(tile, i):
    return jnp.broadcast_to(tile[i:i+1, :], (8, 128))


def factor(m_ref, size, block):
    lanes = size // 128
    tiles = block // 8
    sub = lax.broadcasted_iota(jnp.int32, (8, 128), 0)
    lane = lax.broadcasted_iota(jnp.int32, (8, 128), 1)
    for k in range(size // block):
        base = k * block
        home, shift = base // 128, base % 128
        panel = []
        for t in range(tiles):
            line = [m_ref[base + 8 * t: base + 8 * t + 8, l * 128: l * 128 + 128] for l in range(lanes)]
            line.append(line[home])
            inside = (lane >= shift) & (lane < shift + block)
            line[home] = jnp.where(inside, (lane - shift == sub + 8 * t).astype(F32), line[home])
            panel.append(line)
        done = [[None] * lanes for _ in range(tiles)]
        cols, raw, invs, fronts, seen = [], [], [], {}, {}
        for j in range(block):
            if j in FRONTS:
                lo_c, hi_c = FRONTS[j]
                for c in range(lo_c, hi_c):
                    fronts[c] = [jnp.broadcast_to(panel[t][lanes][:, shift + c: shift + c + 1], (8, 128)) for t in range(c // 8, tiles)]
                    seen[c] = j
            first = j // 8
            col = fronts[j]
            for p in range(seen[j], j):
                if p == j - 1:
                    scale = row_of(raw[p][first - p // 8], j % 8)
                    for t in range(first, tiles):
                        col[t - first] = col[t - first] - raw[p][t - p // 8] * scale * invs[p]
                else:
                    scale = row_of(cols[p][first - p // 8], j % 8)
                    for t in range(first, tiles):
                        col[t - first] = col[t - first] - cols[p][t - p // 8] * scale
            raw.append(col)
            pivot = row_of(col[0], j % 8)
            invs.append(1.0 / pivot)
            inv = lax.rsqrt(pivot)
            col = [c * inv for c in col]
            cols.append(col)
            below = jnp.where(sub > j % 8, col[0], 0.0)
            for l in range(lanes + 1 if j < max(FRONTS) else lanes):
                line = row_of(panel[first][l], j % 8) * inv
                if l < lanes:
                    old = done[first][l]
                    done[first][l] = line if old is None else jnp.where(sub >= j % 8, line, old)
                for t in range(first, tiles):
                    panel[t][l] = panel[t][l] - (below if t == first else col[t - first]) * line
        z = jnp.concatenate([jnp.concatenate(done[t], axis=1) for t in range(tiles)], axis=0)
        m_ref[base: base + block, :] = z
        after = base + block
        if after < size:
            hi, lo = split(z)
            left = jnp.concatenate([hi, hi, lo], axis=0).T
            right = jnp.concatenate([hi, lo, hi], axis=0)
            update = jnp.dot(left[after:], right, preferred_element_type=F32)
            rest = m_ref[after:, :]
            col_id = lax.broadcasted_iota(jnp.int32, rest.shape, 1)
            rest = jnp.where((col_id >= base) & (col_id < after), 0.0, rest)
            m_ref[after:, :] = rest - update


def dot3(a, b, product=dot):
    a_hi, a_lo = split(a)
    b_hi, b_lo = split(b)
    return product(a_hi, b_hi) + product(a_lo, b_hi) + product(a_hi, b_lo)


def update_kernel(fwd_ref, ens_ref, noise_hbm, picks_ref, out_ref, noise_v, m_ref, noise_sem):
    mem = lax.axis_index("mem")
    own = out_ref.shape[0]
    noise_copy = pltpu.make_async_copy(noise_hbm, noise_v, noise_sem)
    noise_copy.start()

    def rows_of(m):
        lines = [[fwd_ref[m, h, r * 2 + l] for h in range(2) for l in range(2)] for r in range(4)]
        return jnp.concatenate([jnp.concatenate(line, axis=1) for line in lines], axis=0)

    forward = jnp.concatenate([rows_of(m) for m in range(8)], axis=0)
    members = forward.shape[0]
    obs_rows, var_rows = picks_ref[0:1, :], picks_ref[1:2, :]
    scale = lax.rsqrt(var_rows)
    spread = (forward - jnp.mean(forward, axis=0, keepdims=True)) * scale
    both = (members, members)
    eye = (lax.broadcasted_iota(jnp.int32, both, 0) == lax.broadcasted_iota(jnp.int32, both, 1)).astype(F32)
    m_ref[...] = dot3(spread, spread, dot_rows) + (members - 1) * eye
    factor(m_ref, members, BLOCK)
    noise_copy.wait()
    residual = (obs_rows + jnp.sqrt(var_rows) * noise_v[...] - rows_of(mem)) * scale
    cross = dot3(residual, spread, dot_rows)
    lower = lax.broadcasted_iota(jnp.int32, both, 0) >= lax.broadcasted_iota(jnp.int32, both, 1)
    inverse = jnp.where(lower, m_ref[...], 0.0)
    weights = dot3(dot3(cross, inverse, dot_rows), inverse)
    weights = weights - jnp.mean(weights, axis=1, keepdims=True)
    own_rows = pl.ds(pl.multiple_of(mem * own, own), own)
    step = 512
    for c in range(out_ref.shape[1] // step):
        part = pl.ds(c * step, step)
        out_ref[:, part] = ens_ref[own_rows, part] + dot3(weights, ens_ref[:, part])


def update(pieces, gathered, noise, picks):
    pieces, gathered, picks = (
        pltpu.with_memory_space_constraint(a, pltpu.VMEM) for a in (pieces, gathered, picks)
    )
    members, params = gathered.shape
    own = noise.shape[0]
    vmem_spec = pl.BlockSpec(memory_space=pltpu.VMEM)
    return pl.pallas_call(
        update_kernel,
        name="update",
        out_shape=jax.ShapeDtypeStruct((own, params), F32),
        in_specs=[vmem_spec, vmem_spec, pl.BlockSpec(memory_space=pl.ANY), vmem_spec],
        out_specs=vmem_spec,
        scratch_shapes=[
            pltpu.VMEM(noise.shape, F32),
            pltpu.VMEM((members, members), F32),
            pltpu.SemaphoreType.DMA,
        ],
    )(pieces, gathered, noise, picks)


def per_device(operator, ensemble, noise, observations, variances, rows):
    obs, var = observations.reshape(128, 128), variances.reshape(128, 128)
    pieces, gathered, picks = exchange(operator, ensemble, obs, var, rows.reshape(1, -1))
    return update(pieces, gathered, noise, picks)


def solution(mesh):
    return jax.shard_map(
        per_device,
        mesh=mesh,
        in_specs=(P("par", None), P("mem", "par"), P("mem", None), P(), P(), P()),
        out_specs=P("mem", "par"),
        check_vma=False,
    )
```

```python
import jax
import jax.numpy as jnp
from jax import lax
from jax.experimental import pallas as pl
from jax.experimental.pallas import tpu as pltpu
from jax.sharding import PartitionSpec as P

MESH = pl.DeviceIdType.MESH
CHUNKS = 4
BLOCK = 32
NEARX = 0
EPOS = 1
SPLIT = 0
FRONTS = {0: (0, 16), 12: (16, 32)}
FAR_FIRST = (4, 3, 5, 2, 6, 1, 7)
NEAR = (1, 7, 2, 6)
FAR = (4, 3, 5)


def slot_of(d):
    return jnp.where(d == 0, 0, jnp.where(d <= 4, 2 * d - 1, 2 * (8 - d)))


SLOTS = (0, 1, 3, 5, 7, 6, 4, 2)
F32 = jnp.float32
BF16 = jnp.bfloat16


def split(a):
    hi = a.astype(BF16)
    return hi, (a - hi.astype(F32)).astype(BF16)


def dot(a, b):
    return jnp.dot(a, b, preferred_element_type=F32)


def dot_rows(a, b):
    return lax.dot_general(a, b, (((1,), (1,)), ((), ())), preferred_element_type=F32)


def picked(tables, rows):
    n = rows.shape[1]
    high, low = rows // 128, rows % 128
    hot = (lax.broadcasted_iota(jnp.int32, (128, n), 0) == high).astype(BF16)
    mask = lax.broadcasted_iota(jnp.int32, (128, n), 0) == low
    out = []
    for table in tables:
        t = table.T
        first = t.astype(BF16)
        t = t - first.astype(F32)
        second = t.astype(BF16)
        third = (t - second.astype(F32)).astype(BF16)
        lines = (dot(first, hot) + dot(second, hot)) + dot(third, hot)
        out.append(jnp.sum(jnp.where(mask, lines, 0.0), axis=0, keepdims=True))
    return out


def exchange_kernel(
    op_hbm, ens_hbm, obs_hbm, var_hbm, rows_hbm, fwd_all, ens_all, picks,
    op_v, obs_v, var_v, rows_v, source, came_one, middle, came_two,
    op_sem, load_sem, send_sem, one_r, two_r, three_r, near_r, far_r, cross_r, twin_r, ens_r, ens_twin_r,
):
    mem = lax.axis_index("mem")
    par = lax.axis_index("par")
    x, core = mem // 2, mem % 2
    y, z = par // 8, par % 8
    own = ens_hbm.shape[0]
    depth = op_hbm.shape[0] // CHUNKS
    twin = x * 2 + (1 - core)

    def at_z(d):
        return (mem, y * 8 + (z + d) % 8)

    def at_y(d):
        return (mem, ((y + d) % 8) * 8 + z)

    def mem_at(d):
        return ((x + d) % 4) * 2 + core

    across, along, place = (at_z, at_y), (at_y, at_z), (z, y)

    def copy_to(src, dst, send, recv, device):
        return pltpu.make_async_remote_copy(
            src_ref=src, dst_ref=dst, send_sem=send, recv_sem=recv, device_id=device, device_id_type=MESH
        )

    def arrived(ref, recv):
        copy_to(ref, ref, send_sem.at[0], recv, (twin, par)).wait_recv()

    def sent(ref, send):
        copy_to(ref, ref, send, one_r.at[0], (twin, par)).wait_send()

    barrier = pltpu.get_barrier_semaphore()
    friends = [at(d) for d in FAR_FIRST for at in across]
    friends += [(((x + d) % 4) * 2 + c, par) for d in (2, 1, 3) for c in range(2)] + [(twin, par)]
    for friend in friends:
        pl.semaphore_signal(barrier, inc=1, device_id=friend, device_id_type=MESH)

    own_rows = pl.ds(pl.multiple_of(mem * own, own), own)
    own_ens = ens_all.at[own_rows]
    ens_copy = pltpu.make_async_copy(ens_hbm, own_ens, load_sem.at[0])
    ens_copy.start()
    op_copies = []
    for c in range(CHUNKS):
        lines = pl.ds(c * depth, depth)
        op_copies.append(pltpu.make_async_copy(op_hbm.at[lines], op_v.at[lines], op_sem.at[c]))
        op_copies[-1].start()
    small = [
        pltpu.make_async_copy(src, dst, load_sem.at[i])
        for i, src, dst in ((1, obs_hbm, obs_v), (2, var_hbm, var_v), (3, rows_hbm, rows_v))
    ]
    for copy in small:
        copy.start()

    ens_copy.wait()

    total = jnp.zeros((own, op_hbm.shape[1]), F32)
    for c in range(CHUNKS):
        op_copies[c].wait()
        op_hi, op_lo = split(op_v[pl.ds(c * depth, depth), :])
        ens_hi, ens_lo = split(ens_all[own_rows, pl.ds(c * depth, depth)])
        total += dot(ens_hi, op_hi) + dot(ens_lo, op_hi) + dot(ens_hi, op_lo)
    for h in range(2):
        for q in range(8):
            top, left = (q // 2) * 8, h * 256 + (q % 2) * 128
            source[h, q] = total[top : top + 8, left : left + 128]

    pl.semaphore_wait(barrier, len(friends))

    for d in FAR_FIRST:
        for h in range(2):
            piece = source.at[h, (place[h] + d) % 8]
            copy_to(piece, came_one.at[h, d], send_sem.at[0], one_r.at[h], across[h](d)).start()
    half = own // 2
    turns = ((0, 1), (1, 3))

    def ens_rows(d, first, count):
        return pl.ds(pl.multiple_of(((x + 4 - d) % 4) * 2 * own + core * own + first, count), count)

    def ens_to_mem(lines, d, recv):
        copy_to(ens_all.at[lines], ens_all.at[lines], send_sem.at[3], ens_r.at[recv], (mem_at(d), par)).start()

    def ens_to_twin(lines):
        copy_to(ens_all.at[lines], ens_all.at[lines], send_sem.at[4], ens_twin_r, (twin, par)).start()

    for i, d in turns:
        ens_to_mem(ens_rows(0, i * half, half), d, d)
    for i, d in turns:
        ens_to_mem(ens_rows(0, (1 - i) * half, half), d, 4 + i)
    copy_to(own_ens, own_ens, send_sem.at[4], ens_twin_r, (twin, par)).start()

    for copy in small:
        copy.wait()
    obs_rows, var_rows = picked((obs_v[...], var_v[...]), rows_v[...])
    picks[...] = jnp.concatenate([obs_rows, var_rows] + [var_rows] * 6, axis=0)

    others = pl.ds(1, 7)
    part = [None, None]
    for h in range(2):
        arrived(came_one.at[h, others], one_r.at[h])
        part[h] = source[h, place[h]]
        for d in range(1, 8):
            part[h] += came_one[h, d]
        middle[h] = part[h]
        for d in FAR_FIRST:
            copy_to(middle.at[h], came_two.at[h, d], send_sem.at[1], two_r.at[h], along[h](d)).start()
    def ens_onward():
        for i, d in turns:
            lines = ens_rows(d, i * half, half)
            arrived(ens_all.at[lines], ens_r.at[d])
            ens_to_mem(lines, d, 2 * i)
            ens_to_twin(lines)

    def ens_rest():
        for i, d in turns:
            lines = ens_rows(d, (1 - i) * half, half)
            arrived(ens_all.at[lines], ens_r.at[4 + i])
            ens_to_twin(lines)

    if EPOS > 0:
        ens_onward()
    for h in range(2):
        arrived(came_two.at[h, others], two_r.at[h])
        for d in range(1, 8):
            part[h] += came_two[h, d]
        fwd_all[mem, h, 0] = part[h]
        for d in FAR_FIRST:
            copy_to(
                fwd_all.at[mem, h, 0], fwd_all.at[mem, h, SLOTS[d]],
                send_sem.at[2], three_r.at[int(d in FAR), h], across[h](d),
            ).start()

    near, far = pl.ds(0, 5), pl.ds(5, 3)

    def mem_from(d):
        return ((x + 4 - d) % 4) * 2 + core

    def blocks(m, slots):
        if SPLIT == 0:
            return [fwd_all.at[m, :, slots]]
        if SPLIT == 1:
            return [fwd_all.at[m, h, slots] for h in range(2)]
        return [fwd_all.at[m, h, i] for i in range(slots.start, slots.start + slots.size) for h in range(2)]

    def to_mem(m, slots, d, send, recv):
        for block in blocks(m, slots):
            copy_to(block, block, send_sem.at[send], recv, (mem_at(d), par)).start()

    def to_twin(m, slots):
        for block in blocks(m, slots):
            copy_to(block, block, send_sem.at[6], twin_r, (twin, par)).start()

    def to_cross(m, slots, d, send, recv):
        for block in blocks(m, slots):
            copy_to(block, block, send_sem.at[send], recv, (((x + d) % 4) * 2 + 1 - core, par)).start()

    if EPOS == 0:
        ens_onward()
    if EPOS != 2:
        ens_rest()
    for h in range(2):
        arrived(fwd_all.at[mem, h, pl.ds(0, 4)], three_r.at[0, h])
    for d in (2, 1, 3):
        to_mem(mem, near, d, 5, near_r.at[d - 1])
        if NEARX:
            to_cross(mem, near, d, 6, twin_r)
    to_twin(mem, near)
    for h in range(2):
        arrived(fwd_all.at[mem, h, far], three_r.at[1, h])
    for d in (2, 1, 3):
        to_mem(mem, far, d, 7, far_r)
        to_cross(mem, far, d, 7, cross_r)
    block = fwd_all.at[mem, :, far]
    copy_to(block, block, send_sem.at[7], cross_r, (twin, par)).start()
    if EPOS == 2:
        ens_rest()
    for d in (1, 3, 2):
        arrived(fwd_all.at[mem_from(d), :, near], near_r.at[d - 1])
        if not NEARX:
            to_twin(mem_from(d), near)
    for i in range(2):
        lines = ens_rows(2, i * half, half)
        arrived(ens_all.at[lines], ens_r.at[2 * i])
        ens_to_twin(lines)
    arrived(fwd_all.at[pl.ds(0, 3), :, far], far_r)
    arrived(fwd_all.at[pl.ds(0, 4), :, far], cross_r)
    arrived(fwd_all.at[pl.ds(0, 4), :, near], twin_r)
    arrived(ens_all.at[pl.ds(0, 4 * own)], ens_twin_r)
    for i in range(2):
        sent(came_one.at[:, others], send_sem.at[i])
    sent(came_one.at[:, others], send_sem.at[2])
    sent(ens_all.at[pl.ds(0, 3 * own)], send_sem.at[3])
    sent(ens_all.at[pl.ds(0, 4 * own)], send_sem.at[4])
    sent(fwd_all.at[pl.ds(0, 3), :, near], send_sem.at[5])
    sent(fwd_all.at[pl.ds(0, 7), :, far], send_sem.at[7])
    sent(fwd_all.at[pl.ds(0, 4), :, near], send_sem.at[6])


def exchange(operator, ensemble, obs, var, rows):
    own, params = ensemble.shape
    width = operator.shape[1]
    any_spec = pl.BlockSpec(memory_space=pl.ANY)
    vmem_spec = pl.BlockSpec(memory_space=pltpu.VMEM)
    dma = pltpu.SemaphoreType.DMA
    return pl.pallas_call(
        exchange_kernel,
        name="exchange",
        out_shape=(
            pltpu.VMEM((8, 2, 8, 8, 128), F32),
            pltpu.VMEM((8 * own, params), F32),
            pltpu.VMEM((8, width), F32),
        ),
        in_specs=[any_spec] * 5,
        out_specs=(vmem_spec,) * 3,
        scratch_shapes=[
            pltpu.VMEM((params, width), F32),
            pltpu.VMEM(obs.shape, F32),
            pltpu.VMEM(var.shape, F32),
            pltpu.VMEM(rows.shape, rows.dtype),
            pltpu.VMEM((2, 8, 8, 128), F32),
            pltpu.VMEM((2, 8, 8, 128), F32),
            pltpu.VMEM((2, 8, 128), F32),
            pltpu.VMEM((2, 8, 8, 128), F32),
            dma((CHUNKS,)), dma((4,)), dma((8,)),
            dma((2,)), dma((2,)), dma((2, 2)), dma((3,)), dma, dma, dma, dma((6,)), dma,
        ],
        compiler_params=pltpu.CompilerParams(collective_id=0, has_side_effects=True),
    )(operator, ensemble, obs, var, rows)


def row_of(tile, i):
    return jnp.broadcast_to(tile[i:i+1, :], (8, 128))


def factor(m_ref, size, block):
    lanes = size // 128
    tiles = block // 8
    sub = lax.broadcasted_iota(jnp.int32, (8, 128), 0)
    lane = lax.broadcasted_iota(jnp.int32, (8, 128), 1)
    for k in range(size // block):
        base = k * block
        home, shift = base // 128, base % 128
        panel = []
        for t in range(tiles):
            line = [m_ref[base + 8 * t: base + 8 * t + 8, l * 128: l * 128 + 128] for l in range(lanes)]
            line.append(line[home])
            inside = (lane >= shift) & (lane < shift + block)
            line[home] = jnp.where(inside, (lane - shift == sub + 8 * t).astype(F32), line[home])
            panel.append(line)
        done = [[None] * lanes for _ in range(tiles)]
        cols, raw, invs, fronts, seen = [], [], [], {}, {}
        for j in range(block):
            if j in FRONTS:
                lo_c, hi_c = FRONTS[j]
                for c in range(lo_c, hi_c):
                    fronts[c] = [jnp.broadcast_to(panel[t][lanes][:, shift + c: shift + c + 1], (8, 128)) for t in range(c // 8, tiles)]
                    seen[c] = j
            first = j // 8
            col = fronts[j]
            for p in range(seen[j], j):
                if p == j - 1:
                    scale = row_of(raw[p][first - p // 8], j % 8)
                    for t in range(first, tiles):
                        col[t - first] = col[t - first] - raw[p][t - p // 8] * scale * invs[p]
                else:
                    scale = row_of(cols[p][first - p // 8], j % 8)
                    for t in range(first, tiles):
                        col[t - first] = col[t - first] - cols[p][t - p // 8] * scale
            raw.append(col)
            pivot = row_of(col[0], j % 8)
            invs.append(1.0 / pivot)
            inv = lax.rsqrt(pivot)
            col = [c * inv for c in col]
            cols.append(col)
            below = jnp.where(sub > j % 8, col[0], 0.0)
            for l in range(lanes + 1 if j < max(FRONTS) else lanes):
                line = row_of(panel[first][l], j % 8) * inv
                if l < lanes:
                    old = done[first][l]
                    done[first][l] = line if old is None else jnp.where(sub >= j % 8, line, old)
                for t in range(first, tiles):
                    panel[t][l] = panel[t][l] - (below if t == first else col[t - first]) * line
        z = jnp.concatenate([jnp.concatenate(done[t], axis=1) for t in range(tiles)], axis=0)
        m_ref[base: base + block, :] = z
        after = base + block
        if after < size:
            hi, lo = split(z)
            left = jnp.concatenate([hi, hi, lo], axis=0).T
            right = jnp.concatenate([hi, lo, hi], axis=0)
            update = jnp.dot(left[after:], right, preferred_element_type=F32)
            rest = m_ref[after:, :]
            col_id = lax.broadcasted_iota(jnp.int32, rest.shape, 1)
            rest = jnp.where((col_id >= base) & (col_id < after), 0.0, rest)
            m_ref[after:, :] = rest - update


def dot3(a, b, product=dot):
    a_hi, a_lo = split(a)
    b_hi, b_lo = split(b)
    return product(a_hi, b_hi) + product(a_lo, b_hi) + product(a_hi, b_lo)


def update_kernel(fwd_ref, ens_ref, noise_hbm, picks_ref, out_hbm, noise_v, m_ref, out_v, noise_sem, out_sem):
    mem = lax.axis_index("mem")
    own = out_hbm.shape[0]
    noise_copy = pltpu.make_async_copy(noise_hbm, noise_v, noise_sem)
    noise_copy.start()

    par = lax.axis_index("par")
    slots = [[slot_of((at + 8 - q) % 8) for q in range(8)] for at in (par % 8, par // 8)]

    def rows_of(m):
        lines = [[fwd_ref[m, h, slots[h][r * 2 + l]] for h in range(2) for l in range(2)] for r in range(4)]
        return jnp.concatenate([jnp.concatenate(line, axis=1) for line in lines], axis=0)

    forward = jnp.concatenate([rows_of(m) for m in range(8)], axis=0)
    members = forward.shape[0]
    obs_rows, var_rows = picks_ref[0:1, :], picks_ref[1:2, :]
    scale = lax.rsqrt(var_rows)
    spread = (forward - jnp.mean(forward, axis=0, keepdims=True)) * scale
    both = (members, members)
    eye = (lax.broadcasted_iota(jnp.int32, both, 0) == lax.broadcasted_iota(jnp.int32, both, 1)).astype(F32)
    m_ref[...] = dot3(spread, spread, dot_rows) + (members - 1) * eye
    factor(m_ref, members, BLOCK)
    noise_copy.wait()
    residual = (obs_rows + jnp.sqrt(var_rows) * noise_v[...] - rows_of(mem)) * scale
    cross = dot3(residual, spread, dot_rows)
    lower = lax.broadcasted_iota(jnp.int32, both, 0) >= lax.broadcasted_iota(jnp.int32, both, 1)
    inverse = jnp.where(lower, m_ref[...], 0.0)
    weights = dot3(dot3(cross, inverse, dot_rows), inverse)
    weights = weights - jnp.mean(weights, axis=1, keepdims=True)
    own_rows = pl.ds(pl.multiple_of(mem * own, own), own)
    step = 512
    copies = []
    for c in range(out_hbm.shape[1] // step):
        part = pl.ds(c * step, step)
        out_v[:, part] = ens_ref[own_rows, part] + dot3(weights, ens_ref[:, part])
        copies.append(pltpu.make_async_copy(out_v.at[:, part], out_hbm.at[:, part], out_sem.at[c]))
        copies[-1].start()
    for copy in copies:
        copy.wait()


def update(pieces, gathered, noise, picks):
    pieces, gathered, picks = (
        pltpu.with_memory_space_constraint(a, pltpu.VMEM) for a in (pieces, gathered, picks)
    )
    members, params = gathered.shape
    own = noise.shape[0]
    vmem_spec = pl.BlockSpec(memory_space=pltpu.VMEM)
    return pl.pallas_call(
        update_kernel,
        name="update",
        out_shape=jax.ShapeDtypeStruct((own, params), F32),
        in_specs=[vmem_spec, vmem_spec, pl.BlockSpec(memory_space=pl.ANY), vmem_spec],
        out_specs=pl.BlockSpec(memory_space=pl.ANY),
        scratch_shapes=[
            pltpu.VMEM(noise.shape, F32),
            pltpu.VMEM((members, members), F32),
            pltpu.VMEM((own, params), F32),
            pltpu.SemaphoreType.DMA,
            pltpu.SemaphoreType.DMA((4,)),
        ],
    )(pieces, gathered, noise, picks)


def per_device(operator, ensemble, noise, observations, variances, rows):
    obs, var = observations.reshape(128, 128), variances.reshape(128, 128)
    pieces, gathered, picks = exchange(operator, ensemble, obs, var, rows.reshape(1, -1))
    return update(pieces, gathered, noise, picks)


def solution(mesh):
    return jax.shard_map(
        per_device,
        mesh=mesh,
        in_specs=(P("par", None), P("mem", "par"), P("mem", None), P(), P(), P()),
        out_specs=P("mem", "par"),
        check_vma=False,
    )
```
